32 devices in a mesh: row: 4 (over z), col: 4 (over y, x), pupil: 2 (over core).
Axes of the slice: x: 2, y: 2, z: 4, core: 2. Of those that a mesh axis runs over, the one named last changes fastest.
Arguments:
- phase: float32 [512, 8192], P('row', 'col'), may hold values from -3.140625 to 3.140625
- band_offsets: int32 [2, 2], P('pupil'), may hold values from 0 to 8191
- depth_codes: int32 [8], replicated, may hold values from -6 to 6
Outputs:
- retina: float32 [8, 512, 512], P('pupil', ('row', 'col'))
The draws below stay inside these ranges and needn't reach their ends.
Inputs may be any that keep to these rules, and one draw needn't show every extreme that they name: `band_offsets`: A band wraps around modulo 8192.
All inputs are finite; a program needn't handle non-finite values.
Results may differ from the reference program's by a relative error of at most 0.0016.
Values sent between devices are 32-bit elements; how exact they have to be, the bound alone decides.
No kernel may reach another device: no remote copies, remote signals or barrier semaphores. Data moves between devices by JAX's collectives and lax.ppermute only.
A program may use at most 64 MiB of HBM per device.

```python
import math
import jax
import jax.numpy as jnp
from jax import lax

HOLO = 8192
BAND = 512
DEPTHS = 8
ROWS = 512
PUPILS = 2


def place_ends(result, key, smallest, largest):
    longest = result.shape.index(max(result.shape))
    spots = []
    for shift in (0, 1):
        where = [jax.random.randint(jax.random.fold_in(key, axis), (), 0, length) for axis, length in enumerate(result.shape)]
        where[longest] = (where[longest] + shift) % result.shape[longest]
        spots.append(tuple(where))
    return result.at[spots[0]].set(smallest).at[spots[1]].set(largest)


def setup_inputs(seed: int = 0) -> dict:
    keys = jax.random.split(jax.random.key(seed), 4)
    phase = jnp.clip(jax.random.uniform(keys[0], (ROWS, HOLO), jnp.float32, -3.140625, 3.140625), -3.140625, 3.140625)
    band_offsets = place_ends(jax.random.randint(keys[1], (PUPILS, 2), 0, HOLO), jax.random.fold_in(keys[1], 1), 0, HOLO - 1).astype(jnp.int32)
    depth_codes = place_ends(jax.random.randint(keys[2], (DEPTHS,), -6, 7), jax.random.fold_in(keys[2], 1), -6, 6).astype(jnp.int32)
    return {"phase": phase, "band_offsets": band_offsets, "depth_codes": depth_codes}


defocus_scale = 0.5

def band_table(offset, count, length, stride):
    freq = (offset + jnp.arange(count, dtype=jnp.int32)) % HOLO
    index = jnp.arange(length, dtype=jnp.int32) * stride
    angle = 2.0 * math.pi / HOLO * (freq[:, None] * index[None, :] % HOLO).astype(jnp.float32)
    return (jnp.cos(angle), -jnp.sin(angle))

def pupil_image(offsets, field_re, field_im, depth_codes):
    hp = lax.Precision.HIGHEST
    fr_re, fr_im = band_table(offsets[1], BAND, HOLO, 1)
    fr_re = fr_re.astype(jnp.bfloat16)
    fr_im = fr_im.astype(jnp.bfloat16)
    fl_re, fl_im = band_table(offsets[0], BAND, ROWS, HOLO // ROWS)
    half_re = jnp.dot(fr_re, field_re.T, preferred_element_type=jnp.float32) - jnp.dot(fr_im, field_im.T, preferred_element_type=jnp.float32)
    half_im = jnp.dot(fr_re, field_im.T, preferred_element_type=jnp.float32) + jnp.dot(fr_im, field_re.T, preferred_element_type=jnp.float32)
    spec_re = (jnp.dot(half_re, fl_re.T, precision=hp) - jnp.dot(half_im, fl_im.T, precision=hp)) / HOLO
    spec_im = (jnp.dot(half_re, fl_im.T, precision=hp) + jnp.dot(half_im, fl_re.T, precision=hp)) / HOLO
    centre = BAND / 2.0
    grid = jnp.arange(BAND, dtype=jnp.float32) - centre
    radius = (grid[:, None] ** 2 + grid[None, :] ** 2) / (centre * centre)
    turn = math.pi * defocus_scale * depth_codes.astype(jnp.float32)[:, None, None] * radius[None, :, :]
    d_re = spec_re[None] * jnp.cos(turn) - spec_im[None] * jnp.sin(turn)
    d_im = spec_re[None] * jnp.sin(turn) + spec_im[None] * jnp.cos(turn)
    index = jnp.arange(BAND, dtype=jnp.int32)
    angle = 2.0 * math.pi / BAND * (index[:, None] * index[None, :] % BAND).astype(jnp.float32)
    g_re = jnp.cos(angle) / math.sqrt(BAND)
    g_im = jnp.sin(angle) / math.sqrt(BAND)
    z_re = jnp.einsum('xu,dvu->dxv', g_re, d_re, precision=hp) - jnp.einsum('xu,dvu->dxv', g_im, d_im, precision=hp)
    z_im = jnp.einsum('xu,dvu->dxv', g_re, d_im, precision=hp) + jnp.einsum('xu,dvu->dxv', g_im, d_re, precision=hp)
    w_re = jnp.einsum('dxv,vy->dxy', z_re, g_re, precision=hp) - jnp.einsum('dxv,vy->dxy', z_im, g_im, precision=hp)
    w_im = jnp.einsum('dxv,vy->dxy', z_re, g_im, precision=hp) + jnp.einsum('dxv,vy->dxy', z_im, g_re, precision=hp)
    return w_re * w_re + w_im * w_im

def reference(phase, band_offsets, depth_codes):
    field_re = jnp.cos(phase).astype(jnp.bfloat16)
    field_im = jnp.sin(phase).astype(jnp.bfloat16)
    images = lax.map(lambda offsets: pupil_image(offsets, field_re, field_im, depth_codes), band_offsets)
    return lax.optimization_barrier(jnp.sum(images, axis=0)) / PUPILS
```

```python
import functools
import math

import jax
import jax.numpy as jnp
from jax import lax
from jax.experimental import pallas as pl
from jax.experimental.pallas import tpu as pltpu
from jax.sharding import PartitionSpec as P

HOLO = 8192
BAND = 512
LANES = 512
STEP = 16
F32 = jnp.float32
BF16 = jnp.bfloat16
I32 = jnp.int32


def turn_parts(r, q):
    z = r * r
    s = ((-1.9515295891e-4 * z + 8.3321608736e-3) * z - 1.6666654611e-1) * z * r + r
    c = ((2.443315711809948e-5 * z - 1.388731625493765e-3) * z + 4.166664568298827e-2) * (z * z) - 0.5 * z + 1.0
    odd = (q & 1) == 1
    cs = jnp.where(odd, s, c)
    sn = jnp.where(odd, c, s)
    return jnp.where(((q + 1) & 2) == 2, -cs, cs), jnp.where((q & 2) == 2, -sn, sn)


def circle(k, size):
    quarter = size // 4
    k = k + quarter // 2
    q = k >> (quarter.bit_length() - 1)
    r = (k & (quarter - 1)) - quarter // 2
    return turn_parts(r.astype(F32) * (2.0 * math.pi / size), q)


def radians(x):
    qf = jnp.floor(x * (2.0 / math.pi) + 0.5)
    r = ((x - qf * 1.5703125) - qf * 4.837512969970703125e-4) - qf * 7.54978995489188216e-8
    return turn_parts(r, qf.astype(I32))


def split(x):
    hi = x.astype(BF16)
    return hi, (x - hi.astype(F32)).astype(BF16)


def mm(a, b, nt=False):
    dims = (((1,), (1 if nt else 0,)), ((), ()))
    return lax.dot_general(a, b, dims, preferred_element_type=F32)


def mm3(ah, al, bh, bl, nt=False):
    return mm(ah, bh, nt) + (mm(al, bh, nt) + mm(ah, bl, nt))


def half_kernel(n_col, offs, ph, *refs):
    outs = refs[:n_col]
    field, table, a_re, a_im, b_re, b_im = refs[n_col:]
    rows, cols = ph.shape
    share = BAND // n_col
    offset, me = offs[0, 1], lax.axis_index("col")
    n0 = me * cols
    per = share // STEP

    def fill(i, _):
        at = pl.multiple_of(i * STEP, STEP)
        for j in range(0, cols, LANES):
            c, s = radians(ph[pl.ds(at, STEP), j : j + LANES])
            field[pl.ds(at, STEP), j : j + LANES] = c.astype(BF16)
            field[pl.ds(rows + at, STEP), j : j + LANES] = s.astype(BF16)
        return 0

    lax.fori_loop(0, rows // STEP, fill, 0)
    for j in range(0, cols, LANES):
        n = n0 + j + lax.broadcasted_iota(I32, (STEP, LANES), 1)
        low = lax.broadcasted_iota(I32, (STEP, LANES), 0)
        c, s = circle((low * n) & (HOLO - 1), HOLO)
        b_re[:, j : j + LANES] = c
        b_im[:, j : j + LANES] = -s
        n = n0 + j + lax.broadcasted_iota(I32, (n_col * per, LANES), 1)
        row = lax.broadcasted_iota(I32, (n_col * per, LANES), 0)
        block = me ^ (row // per)
        v = block * share + (row % per) * STEP
        c, s = circle((((offset + v) & (HOLO - 1)) * n) & (HOLO - 1), HOLO)
        a_re[:, j : j + LANES] = c
        a_im[:, j : j + LANES] = -s
    for t in list(range(1, n_col)) + [0]:
        buf = table.at[t % 2]
        for j in range(0, cols, LANES):
            br = b_re[:, j : j + LANES]
            bi = b_im[:, j : j + LANES]
            for h in range(per):
                ar = a_re[t * per + h : t * per + h + 1, j : j + LANES]
                ai = a_im[t * per + h : t * per + h + 1, j : j + LANES]
                buf[h * STEP : (h + 1) * STEP, j : j + LANES] = (ar * br - ai * bi).astype(BF16)
                buf[share + h * STEP : share + (h + 1) * STEP, j : j + LANES] = (ar * bi + ai * br).astype(BF16)
        prod = mm(buf[...], field[...], nt=True)
        outs[t][:share, :] = prod[:share, :rows] - prod[share:, rows:]
        outs[t][share:, :] = prod[:share, rows:] + prod[share:, :rows]


def rows_kernel(n_row, n_col, n_pupil, depths, spacing, offs, codes, fl_hi, fl_lo, lens_hi, lens_lo, ev):
    offset = offs[0, 0]
    r, c, p = (lax.axis_index(a) for a in ("row", "col", "pupil"))
    own = depths // n_pupil
    code = [codes[((d // own) ^ p) * own + d % own] for d in range(depths)]
    rows_here = fl_hi.shape[0] // n_row
    xs = BAND // (n_row * n_col)
    share = BAND // n_col
    big = 4 * (BAND // 2) ** 2
    chunk = 32

    def fill(i, _):
        at = pl.multiple_of(i * chunk, chunk)
        row = at + lax.broadcasted_iota(I32, (chunk, BAND), 0)
        u = lax.broadcasted_iota(I32, (chunk, BAND), 1)
        m = (r ^ (row // rows_here)) * rows_here + row % rows_here
        k = (((offset + u) & (HOLO - 1)) * ((m * spacing) & (HOLO - 1))) & (HOLO - 1)
        cs, sn = circle(k, HOLO)
        hi, lo = split(cs)
        fl_hi[pl.ds(at, chunk), :BAND] = hi
        fl_lo[pl.ds(at, chunk), :BAND] = lo
        hi, lo = split(-sn)
        fl_hi[pl.ds(at, chunk), BAND:] = hi
        fl_lo[pl.ds(at, chunk), BAND:] = lo
        return 0

    lax.fori_loop(0, n_row * rows_here // chunk, fill, 0)

    scale = 1.0 / math.sqrt(BAND)
    u = lax.broadcasted_iota(I32, (1, BAND), 1) - BAND // 2
    v = c * share + lax.broadcasted_iota(I32, (1, share), 1) - BAND // 2
    for t in range(n_col):
        x = (r * n_col + (c ^ t)) * xs + lax.broadcasted_iota(I32, (xs, BAND), 0)
        uu = lax.broadcasted_iota(I32, (xs, BAND), 1)
        g_re, g_im = circle((x * uu) & (BAND - 1), BAND)
        g_re = g_re * scale
        g_im = g_im * scale
        for d in range(depths):
            e_re, e_im = circle((code[d] * (u * u)) & (big - 1), big)
            re = g_re * e_re - g_im * e_im
            im = g_re * e_im + g_im * e_re
            at = (t * depths + d) * xs
            hi, lo = split(re)
            lens_hi[at : at + xs, :BAND] = hi
            lens_lo[at : at + xs, :BAND] = lo
            hi, lo = split(im)
            lens_hi[at : at + xs, BAND:] = hi
            lens_lo[at : at + xs, BAND:] = lo
    for d in range(depths):
        e_re, e_im = circle((code[d] * (v * v)) & (big - 1), big)
        ev[d : d + 1, :share] = e_re
        ev[d : d + 1, share:] = e_im


def image_table_kernel(n_col, g_hi, g_lo):
    c = lax.axis_index("col")
    share = BAND // n_col
    chunk = 32
    scale = 1.0 / math.sqrt(BAND)

    def fill(i, _):
        at = pl.multiple_of(i * chunk, chunk)
        row = at + lax.broadcasted_iota(I32, (chunk, BAND), 0)
        y = lax.broadcasted_iota(I32, (chunk, BAND), 1)
        v = (c ^ (row // share)) * share + row % share
        cs, sn = circle((v * y) & (BAND - 1), BAND)
        hi, lo = split(cs * scale)
        g_hi[pl.ds(at, chunk), :BAND] = hi
        g_lo[pl.ds(at, chunk), :BAND] = lo
        hi, lo = split(sn * scale)
        g_hi[pl.ds(at, chunk), BAND:] = hi
        g_lo[pl.ds(at, chunk), BAND:] = lo
        return 0

    lax.fori_loop(0, BAND // chunk, fill, 0)


def lens_kernel(n_row, n_col, depths, *refs):
    halves = refs[:n_row]
    fl_hi, fl_lo, lens_hi, lens_lo, ev = refs[n_row : n_row + 5]
    outs = refs[n_row + 5 : n_row + 5 + n_col]
    w_hi, w_lo = refs[n_row + 5 + n_col :]
    share = BAND // n_col
    xs = BAND // (n_row * n_col)
    x = jnp.concatenate([h[...] for h in halves], axis=1)
    hi, lo = split(x)
    s = mm3(hi, lo, fl_hi[...], fl_lo[...])
    s_re = (s[:share, :BAND] - s[share:, BAND:]) * (1.0 / HOLO)
    s_im = (s[:share, BAND:] + s[share:, :BAND]) * (1.0 / HOLO)
    hi, lo = split(s_re)
    w_hi[:share, :BAND] = hi
    w_lo[:share, :BAND] = lo
    w_hi[share:, BAND:] = hi
    w_lo[share:, BAND:] = lo
    hi, lo = split(s_im)
    w_hi[share:, :BAND] = hi
    w_lo[share:, :BAND] = lo
    w_hi[:share, BAND:] = -hi
    w_lo[:share, BAND:] = -lo
    block = depths * xs
    for t in list(range(1, n_col)) + [0]:
        at = t * block
        z = mm3(lens_hi[at : at + block, :], lens_lo[at : at + block, :], w_hi[...], w_lo[...], nt=True)
        for d in range(depths):
            re = z[d * xs : (d + 1) * xs, :share]
            im = z[d * xs : (d + 1) * xs, share:]
            e_re = ev[d : d + 1, :share]
            e_im = ev[d : d + 1, share:]
            outs[t][d * xs : (d + 1) * xs, :] = re * e_re - im * e_im
            outs[t][block + d * xs : block + (d + 1) * xs, :] = re * e_im + im * e_re


def image_kernel(n_col, n_pupil, *refs):
    blocks = refs[:n_col]
    g_hi, g_lo = refs[n_col : n_col + 2]
    outs = refs[n_col + 2 :]
    x = jnp.concatenate([b[...] for b in blocks], axis=1)
    hi, lo = split(x)
    z = mm3(hi, lo, g_hi[...], g_lo[...])
    n = x.shape[0] // 2
    re = z[:n, :BAND] - z[n:, BAND:]
    im = z[:n, BAND:] + z[n:, :BAND]
    power = re * re + im * im
    m = n // n_pupil
    for t in range(n_pupil):
        outs[t][...] = power[t * m : (t + 1) * m]


def spec(shape, dtype=F32):
    return jax.ShapeDtypeStruct(shape, dtype)


def call(kernel, outs, smem, scratch=(), n_in=0):
    vm = pl.BlockSpec(memory_space=pltpu.VMEM)
    return pl.pallas_call(
        kernel,
        out_shape=outs,
        in_specs=[pl.BlockSpec(memory_space=pltpu.SMEM)] * smem + [vm] * n_in,
        out_specs=[vm] * len(outs),
        scratch_shapes=list(scratch),
        compiler_params=pltpu.CompilerParams(vmem_limit_bytes=48 * 1024 * 1024),
    )


def swap(x, axis, t):
    n = lax.axis_size(axis)
    return lax.ppermute(x, axis, [(i, i ^ t) for i in range(n)])


def local(phase, band_offsets, depth_codes):
    rows, cols = phase.shape
    n_row, n_col, n_pupil = (lax.axis_size(a) for a in ("row", "col", "pupil"))
    depths = depth_codes.shape[0]
    own = depths // n_pupil
    share = BAND // n_col
    xs = BAND // (n_row * n_col)
    block = depths * xs
    spacing = HOLO // (rows * n_row)

    part = call(
        functools.partial(half_kernel, n_col),
        [spec((2 * share, rows))] * n_col,
        1,
        [
            pltpu.VMEM((2 * rows, cols), BF16),
            pltpu.VMEM((2, 2 * share, cols), BF16),
            pltpu.VMEM((BAND // STEP, cols), F32),
            pltpu.VMEM((BAND // STEP, cols), F32),
            pltpu.VMEM((STEP, cols), F32),
            pltpu.VMEM((STEP, cols), F32),
        ],
        1,
    )(band_offsets, phase)
    got = [swap(part[t], "col", t) for t in range(n_col - 1, 0, -1)]

    fl_hi, fl_lo, lens_hi, lens_lo, ev = call(
        functools.partial(rows_kernel, n_row, n_col, n_pupil, depths, spacing),
        [
            spec((n_row * rows, 2 * BAND), BF16),
            spec((n_row * rows, 2 * BAND), BF16),
            spec((n_col * block, 2 * BAND), BF16),
            spec((n_col * block, 2 * BAND), BF16),
            spec((depths, 2 * share)),
        ],
        2,
    )(band_offsets, depth_codes)
    g_hi, g_lo = call(
        functools.partial(image_table_kernel, n_col),
        [spec((BAND, 2 * BAND), BF16)] * 2,
        0,
    )()

    half = part[0]
    for h in got:
        half = half + h
    halves = [half] + [swap(half, "row", t) for t in range(1, n_row)]
    lens = call(
        functools.partial(lens_kernel, n_row, n_col, depths),
        [spec((2 * block, share))] * n_col,
        0,
        [pltpu.VMEM((2 * share, 2 * BAND), BF16)] * 2,
        n_row + 5,
    )(*halves, fl_hi, fl_lo, lens_hi, lens_lo, ev)
    blocks = [lens[0]] + [swap(lens[t], "col", t) for t in range(n_col - 1, 0, -1)][::-1]
    power = call(
        functools.partial(image_kernel, n_col, n_pupil),
        [spec((block // n_pupil, BAND))] * n_pupil,
        0,
        (),
        n_col + 2,
    )(*blocks, g_hi, g_lo)
    total = power[0]
    for t in range(1, n_pupil):
        total = total + swap(power[t], "pupil", t)
    total = total * (1.0 / (band_offsets.shape[0] * n_pupil))
    return total.reshape(own, xs, BAND)


def solution(mesh):
    in_specs = (P("row", "col"), P("pupil", None), P())
    out_specs = P("pupil", ("row", "col"), None)
    return jax.shard_map(local, mesh=mesh, in_specs=in_specs, out_specs=out_specs, check_vma=False)
```

```python
import functools
import math

import jax
import jax.numpy as jnp
from jax import lax
from jax.experimental import pallas as pl
from jax.experimental.pallas import tpu as pltpu
from jax.sharding import PartitionSpec as P


HOLO = 8192
BAND = 512
LANES = 512
STEP = 16
CHUNKS = 2
F32 = jnp.float32
BF16 = jnp.bfloat16
I32 = jnp.int32


def turn_parts(r, q):
    z = r * r
    s = ((-1.9515295891e-4 * z + 8.3321608736e-3) * z - 1.6666654611e-1) * z * r + r
    c = ((2.443315711809948e-5 * z - 1.388731625493765e-3) * z + 4.166664568298827e-2) * (z * z) - 0.5 * z + 1.0
    odd = (q & 1) == 1
    cs = jnp.where(odd, s, c)
    sn = jnp.where(odd, c, s)
    return jnp.where(((q + 1) & 2) == 2, -cs, cs), jnp.where((q & 2) == 2, -sn, sn)


def circle(k, size):
    quarter = size // 4
    k = k + quarter // 2
    q = k >> (quarter.bit_length() - 1)
    r = (k & (quarter - 1)) - quarter // 2
    return turn_parts(r.astype(F32) * (2.0 * math.pi / size), q)


def poly(z, *coefficients):
    total = coefficients[-1] * z + coefficients[-2]
    for c in coefficients[-3::-1]:
        total = total * z + c
    return total


def radians(x):
    h = 0.5 * x
    z = h * h
    s = h * poly(z, 1.0, -0.1666666716337204, 0.008333330973982811, -0.00019840861205011606, 2.752528644123231e-06, -2.3889498379503493e-08)
    c = poly(z, 1.0, -0.5, 0.0416666679084301, -0.0013888884568586946, 2.4801040126476437e-05, -2.75246833325582e-07, 1.9907673287633543e-09)
    t = s + s
    return 1.0 - t * s, t * c


def split(x):
    hi = x.astype(BF16)
    return hi, (x - hi.astype(F32)).astype(BF16)


def mm(a, b, nt=False):
    dims = (((1,), (1 if nt else 0,)), ((), ()))
    return lax.dot_general(a, b, dims, preferred_element_type=F32)


def rotate(a_re, a_im, b_re, b_im):
    return a_re * b_re - a_im * b_im, a_re * b_im + a_im * b_re


def put(hi_ref, lo_ref, at, size, col, x):
    hi, lo = split(x)
    hi_ref[pl.ds(at, size), col : col + BAND] = hi
    lo_ref[pl.ds(at, size), col : col + BAND] = lo
    return hi, lo


def multiply_band(n_col, t, table, field, a_re, a_im, b_re, b_im, out):
    rows = field.shape[0] // 2
    cols = field.shape[1]
    part = BAND // (n_col * CHUNKS)
    per = part // STEP
    for j in range(0, cols, LANES):
        br = b_re[:, j : j + LANES]
        bi = b_im[:, j : j + LANES]
        for h in range(CHUNKS):
            for i in range(per):
                row = (t * CHUNKS + h) * per + i
                re, im = rotate(a_re[row : row + 1, j : j + LANES], a_im[row : row + 1, j : j + LANES], br, bi)
                at = 2 * h * part + i * STEP
                table[at : at + STEP, j : j + LANES] = re.astype(BF16)
                table[at + part : at + part + STEP, j : j + LANES] = im.astype(BF16)
    prod = mm(table[...], field[...], nt=True)
    for at in range(0, 2 * CHUNKS * part, 2 * part):
        mid = at + part
        out[at:mid, :] = prod[at:mid, :rows] - prod[mid : mid + part, rows:]
        out[mid : mid + part, :] = prod[at:mid, rows:] + prod[mid : mid + part, :rows]


def first_kernel(n_col, offs_hbm, ph_hbm, out, field, a_re, a_im, b_re, b_im, ph, offs, table, sem, ph_sem):
    rows, cols = ph.shape
    pieces = ph_sem.shape[0]
    size = rows // pieces
    get = pltpu.make_async_copy(offs_hbm, offs, sem)
    get.start()
    loads = [
        pltpu.make_async_copy(ph_hbm.at[pl.ds(i * size, size)], ph.at[pl.ds(i * size, size)], ph_sem.at[i])
        for i in range(pieces)
    ]
    for load in loads:
        load.start()
    me = lax.axis_index("col")
    n0 = me * cols
    share = BAND // n_col
    per = share // STEP
    for j in range(0, cols, LANES):
        n = n0 + j + lax.broadcasted_iota(I32, (STEP, LANES), 1)
        low = lax.broadcasted_iota(I32, (STEP, LANES), 0)
        c, s = circle((low * n) & (HOLO - 1), HOLO)
        b_re[:, j : j + LANES] = c
        b_im[:, j : j + LANES] = -s
    for i in range(pieces):
        loads[i].wait()
        for at in range(i * size, (i + 1) * size, STEP):
            for j in range(0, cols, LANES):
                c, s = radians(ph[at : at + STEP, j : j + LANES])
                field[at : at + STEP, j : j + LANES] = c.astype(BF16)
                field[rows + at : rows + at + STEP, j : j + LANES] = s.astype(BF16)
    get.wait()
    offset = offs[0, 1]
    for j in range(0, cols, LANES):
        n = n0 + j + lax.broadcasted_iota(I32, (BAND // STEP, LANES), 1)
        row = lax.broadcasted_iota(I32, (BAND // STEP, LANES), 0)
        v = (me ^ (row // per)) * share + (row % per) * STEP
        c, s = circle((((offset + v) & (HOLO - 1)) * n) & (HOLO - 1), HOLO)
        a_re[:, j : j + LANES] = c
        a_im[:, j : j + LANES] = -s
    multiply_band(n_col, n_col - 1, table, field, a_re, a_im, b_re, b_im, out)


def later_kernel(n_col, t, field, a_re, a_im, b_re, b_im, out, table):
    multiply_band(n_col, t, table, field, a_re, a_im, b_re, b_im, out)


def lens_table_kernel(
    n_row, n_col, n_pupil, spacing, offs_hbm, codes_hbm, fl_hi, fl_lo, lens_hi, lens_lo, ev, a_re, a_im, offs, codes, sems
):
    gets = [
        pltpu.make_async_copy(offs_hbm, offs, sems.at[0]),
        pltpu.make_async_copy(codes_hbm, codes, sems.at[1]),
    ]
    for get in gets:
        get.start()
    depths = codes.shape[0]
    r, c, p = (lax.axis_index(a) for a in ("row", "col", "pupil"))
    own = depths // n_pupil
    xs = BAND // (n_row * n_col)
    share = BAND // n_col
    part = share // CHUNKS
    big = 4 * (BAND // 2) ** 2
    scale = 1.0 / math.sqrt(BAND)
    for get in gets:
        get.wait()
    offset = offs[0, 0]
    rows_here = fl_hi.shape[0] // n_row
    per = rows_here // STEP
    blocks = a_re.shape[0]
    row = lax.broadcasted_iota(I32, (blocks, BAND), 0)
    freq = (offset + lax.broadcasted_iota(I32, (blocks, BAND), 1)) & (HOLO - 1)
    m = (r ^ (row // per)) * rows_here + (row % per) * STEP
    cs, sn = circle((freq * (m * spacing)) & (HOLO - 1), HOLO)
    a_re[...] = cs
    a_im[...] = -sn
    low = lax.broadcasted_iota(I32, (STEP, BAND), 0)
    freq = (offset + lax.broadcasted_iota(I32, (STEP, BAND), 1)) & (HOLO - 1)
    b_re, b_im = circle((freq * (low * spacing)) & (HOLO - 1), HOLO)
    b_im = -b_im

    def fill(i, _):
        at = pl.multiple_of(i * STEP, STEP)
        re, im = rotate(a_re[pl.ds(i, 1), :], a_im[pl.ds(i, 1), :], b_re, b_im)
        put(fl_hi, fl_lo, at, STEP, 0, re)
        put(fl_hi, fl_lo, at, STEP, BAND, im)
        return 0

    lax.fori_loop(0, blocks, fill, 0, unroll=4)
    code = [codes[((d // own) ^ p) * own + d % own] for d in range(depths)]
    u = lax.broadcasted_iota(I32, (1, BAND), 1) - BAND // 2
    turn = [circle((code[d] * (u * u)) & (big - 1), big) for d in range(depths)]
    for t in range(n_col):
        x = (r * n_col + (c ^ t)) * xs + lax.broadcasted_iota(I32, (xs, BAND), 0)
        uu = lax.broadcasted_iota(I32, (xs, BAND), 1)
        g_re, g_im = circle((x * uu) & (BAND - 1), BAND)
        g_re = g_re * scale
        g_im = g_im * scale
        for d in range(depths):
            re, im = rotate(g_re, g_im, *turn[d])
            at = (t * depths + d) * xs
            put(lens_hi, lens_lo, at, xs, 0, re)
            put(lens_hi, lens_lo, at, xs, BAND, im)
    lane = lax.broadcasted_iota(I32, (1, 2 * part), 1)
    for h in range(CHUNKS):
        v = c * share + h * part + lane % part - BAND // 2
        for d in range(depths):
            e_re, e_im = circle((code[d] * (v * v)) & (big - 1), big)
            at = 2 * (h * depths + d)
            ev[at : at + 1, :] = e_re
            ev[at + 1 : at + 2, :] = jnp.where(lane < part, -e_im, e_im)


def image_table_kernel(n_col, *refs):
    c = lax.axis_index("col")
    share = BAND // n_col
    part = share // CHUNKS
    per = part // STEP
    scale = 1.0 / math.sqrt(BAND)
    a_re, a_im = refs[2 * CHUNKS :]
    row = lax.broadcasted_iota(I32, a_re.shape, 0)
    y = lax.broadcasted_iota(I32, a_re.shape, 1)
    v = (c ^ ((row // per) % n_col)) * share + (row // (per * n_col)) * part + (row % per) * STEP
    cs, sn = circle((v * y) & (BAND - 1), BAND)
    a_re[...] = cs
    a_im[...] = sn
    low = lax.broadcasted_iota(I32, (STEP, BAND), 0)
    y = lax.broadcasted_iota(I32, (STEP, BAND), 1)
    b_re, b_im = circle((low * y) & (BAND - 1), BAND)
    b_re = b_re * scale
    b_im = b_im * scale
    for h in range(CHUNKS):
        g_hi, g_lo = refs[2 * h : 2 * h + 2]
        for t in range(n_col):
            for i in range(per):
                row = (h * n_col + t) * per + i
                re, im = rotate(a_re[row : row + 1, :], a_im[row : row + 1, :], b_re, b_im)
                at = 2 * t * part + i * STEP
                hi, lo = put(g_hi, g_lo, at, STEP, 0, re)
                g_hi[at + part : at + part + STEP, BAND:] = hi
                g_lo[at + part : at + part + STEP, BAND:] = lo
                hi, lo = put(g_hi, g_lo, at, STEP, BAND, im)
                g_hi[at + part : at + part + STEP, :BAND] = -hi
                g_lo[at + part : at + part + STEP, :BAND] = -lo


def lens_kernel(n_row, n_col, depths, chunk, *refs):
    halves = refs[:n_row]
    fl_hi, fl_lo, lens_hi, lens_lo, ev = refs[n_row : n_row + 5]
    outs = refs[n_row + 5 : n_row + 5 + n_col]
    x2, w2 = refs[n_row + 5 + n_col :]
    part = BAND // (n_col * CHUNKS)
    both = 2 * part
    xs = BAND // (n_row * n_col)
    rows_here = halves[0].shape[1]
    for i, h in enumerate(halves):
        hi, lo = split(h[...])
        x2[:both, i * rows_here : (i + 1) * rows_here] = hi
        x2[both:, i * rows_here : (i + 1) * rows_here] = lo
    s = mm(x2[...], fl_hi[...])
    s = s[:both] + (s[both:] + mm(x2[:both, :], fl_lo[...]))
    s_re = (s[:part, :BAND] - s[part:, BAND:]) * (1.0 / HOLO)
    s_im = (s[:part, BAND:] + s[part:, :BAND]) * (1.0 / HOLO)
    hi, lo = split(s_re)
    w2[:part, :BAND] = hi
    w2[part:both, BAND:] = hi
    w2[both : both + part, :BAND] = lo
    w2[both + part :, BAND:] = lo
    hi, lo = split(s_im)
    w2[part:both, :BAND] = hi
    w2[:part, BAND:] = -hi
    w2[both + part :, :BAND] = lo
    w2[both : both + part, BAND:] = -lo
    block = depths * xs
    for t in list(range(1, n_col)) + [0]:
        at = t * block
        z = mm(lens_hi[at : at + block, :], w2[...], nt=True)
        z = z[:, :both] + (z[:, both:] + mm(lens_lo[at : at + block, :], w2[:both, :], nt=True))
        for d in range(depths):
            piece = z[d * xs : (d + 1) * xs, :]
            row = 2 * (chunk * depths + d)
            turned = piece * ev[row : row + 1, :] + pltpu.roll(piece, part, 1) * ev[row + 1 : row + 2, :]
            outs[t][d * xs : (d + 1) * xs, :] = turned


def image_sum(blocks, g_hi, g_lo, lo_rows, hi_rows):
    x = jnp.concatenate([b[lo_rows:hi_rows, :] for b in blocks], axis=1)
    hi, lo = split(x)
    return mm(hi, g_hi[...]) + (mm(lo, g_hi[...]) + mm(hi, g_lo[...]))


def image_kernel(n_col, *refs):
    refs[-1][...] = image_sum(refs[:n_col], refs[n_col], refs[n_col + 1], 0, refs[0].shape[0])


def power_kernel(n_col, lo_rows, hi_rows, *refs):
    z = image_sum(refs[:n_col], refs[n_col], refs[n_col + 1], lo_rows, hi_rows)
    for more in refs[n_col + 2 : -1]:
        z = z + more[lo_rows:hi_rows, :]
    re = z[:, :BAND]
    im = z[:, BAND:]
    refs[-1][...] = re * re + im * im


def spec(shape, dtype=F32):
    return jax.ShapeDtypeStruct(shape, dtype)


def call(kernel, outs, ins, scratch=(), hbm=0, mib=16):
    vm = pl.BlockSpec(memory_space=pltpu.VMEM)
    return pl.pallas_call(
        kernel,
        out_shape=outs,
        in_specs=[pl.BlockSpec(memory_space=pltpu.HBM)] * hbm + [vm] * (ins - hbm),
        out_specs=[vm] * len(outs),
        scratch_shapes=list(scratch),
        compiler_params=pltpu.CompilerParams(vmem_limit_bytes=mib * 1024 * 1024),
    )


def in_hbm(x):
    return pltpu.with_memory_space_constraint(x, pltpu.HBM)


def swap(x, axis, t):
    n = lax.axis_size(axis)
    return lax.ppermute(x, axis, [(i, i ^ t) for i in range(n)])


def local(phase, band_offsets, depth_codes):
    rows, cols = phase.shape
    n_row, n_col, n_pupil = (lax.axis_size(a) for a in ("row", "col", "pupil"))
    depths = depth_codes.shape[0]
    own = depths // n_pupil
    share = BAND // n_col
    part = share // CHUNKS
    xs = BAND // (n_row * n_col)
    block = depths * xs
    spacing = HOLO // (rows * n_row)
    dma = pltpu.SemaphoreType.DMA
    away = range(n_col - 1, 0, -1)

    piece = spec((2 * share, rows))
    table = pltpu.VMEM((2 * share, cols), BF16)
    offs = in_hbm(band_offsets)
    first = call(
        functools.partial(first_kernel, n_col),
        [piece, spec((2 * rows, cols), BF16)] + [spec((BAND // STEP, cols))] * 2 + [spec((STEP, cols))] * 2,
        2,
        [pltpu.VMEM((rows, cols), F32), pltpu.SMEM(band_offsets.shape, I32), table, dma, dma((4,))],
        2,
    )(offs, in_hbm(phase))
    got = [swap(first[0], "col", n_col - 1)]
    for t in range(n_col - 2, -1, -1):
        x = call(functools.partial(later_kernel, n_col, t), [piece], 5, [table])(*first[1:])[0]
        got.append(swap(x, "col", t) if t else x)

    blocks = n_row * rows // STEP
    lens_tables = call(
        functools.partial(lens_table_kernel, n_row, n_col, n_pupil, spacing),
        [spec((n_row * rows, 2 * BAND), BF16)] * 2
        + [spec((n_col * block, 2 * BAND), BF16)] * 2
        + [spec((2 * CHUNKS * depths, 2 * part))],
        2,
        [pltpu.VMEM((blocks, BAND), F32)] * 2
        + [pltpu.SMEM(band_offsets.shape, I32), pltpu.SMEM(depth_codes.shape, I32), dma((2,))],
        2,
    )
    tables = lens_tables(offs, in_hbm(depth_codes))
    image_tables = call(
        functools.partial(image_table_kernel, n_col),
        [spec((2 * n_col * part, 2 * BAND), BF16)] * (2 * CHUNKS),
        0,
        [pltpu.VMEM((BAND // STEP, BAND), F32)] * 2,
    )()

    sums = []
    blocks = []
    for h in range(CHUNKS):
        half = got[-1][2 * h * part : 2 * (h + 1) * part]
        for x in got[:-1]:
            half = half + x[2 * h * part : 2 * (h + 1) * part]
        halves = [half] + [swap(half, "row", t) for t in range(1, n_row)]
        lens = call(
            functools.partial(lens_kernel, n_row, n_col, depths, h),
            [spec((block, 2 * part))] * n_col,
            n_row + 5,
            [pltpu.VMEM((4 * part, n_row * rows), BF16), pltpu.VMEM((4 * part, 2 * BAND), BF16)],
        )(*halves, *tables)
        blocks.append([lens[0]] + [swap(lens[t], "col", t) for t in away][::-1])
    for h in range(CHUNKS - 1):
        sums.append(
            call(functools.partial(image_kernel, n_col), [spec((block, 2 * BAND))], n_col + 2)(
                *blocks[h], *image_tables[2 * h : 2 * h + 2]
            )[0]
        )
    size = block // n_pupil
    power = {}
    for t in list(range(1, n_pupil)) + [0]:
        power[t] = call(
            functools.partial(power_kernel, n_col, t * size, (t + 1) * size),
            [spec((size, BAND))],
            n_col + 2 + len(sums),
        )(*blocks[-1], *image_tables[-2:], *sums)[0]
    total = power[0]
    for t in range(1, n_pupil):
        total = total + swap(power[t], "pupil", t)
    total = total * (1.0 / (band_offsets.shape[0] * n_pupil))
    return total.reshape(own, xs, BAND)


def solution(mesh):
    in_specs = (P("row", "col"), P("pupil", None), P())
    out_specs = P("pupil", ("row", "col"), None)
    return jax.shard_map(local, mesh=mesh, in_specs=in_specs, out_specs=out_specs, check_vma=False)
```

```python
import functools
import math

import jax
import jax.numpy as jnp
from jax import lax
from jax.experimental import pallas as pl
from jax.experimental.pallas import tpu as pltpu
from jax.sharding import PartitionSpec as P


HOLO = 8192
BAND = 512
LANES = 512
STEP = 16
CHUNKS = 2
F32 = jnp.float32
BF16 = jnp.bfloat16
I32 = jnp.int32


def turn_parts(r, q):
    z = r * r
    s = ((-1.9515295891e-4 * z + 8.3321608736e-3) * z - 1.6666654611e-1) * z * r + r
    c = ((2.443315711809948e-5 * z - 1.388731625493765e-3) * z + 4.166664568298827e-2) * (z * z) - 0.5 * z + 1.0
    odd = (q & 1) == 1
    cs = jnp.where(odd, s, c)
    sn = jnp.where(odd, c, s)
    return jnp.where(((q + 1) & 2) == 2, -cs, cs), jnp.where((q & 2) == 2, -sn, sn)


def circle(k, size):
    quarter = size // 4
    k = k + quarter // 2
    q = k >> (quarter.bit_length() - 1)
    r = (k & (quarter - 1)) - quarter // 2
    return turn_parts(r.astype(F32) * (2.0 * math.pi / size), q)


def poly(z, *coefficients):
    total = coefficients[-1] * z + coefficients[-2]
    for c in coefficients[-3::-1]:
        total = total * z + c
    return total


def radians(x):
    h = 0.5 * x
    z = h * h
    s = h * poly(z, 1.0, -0.1666666716337204, 0.008333330973982811, -0.00019840861205011606, 2.752528644123231e-06, -2.3889498379503493e-08)
    c = poly(z, 1.0, -0.5, 0.0416666679084301, -0.0013888884568586946, 2.4801040126476437e-05, -2.75246833325582e-07, 1.9907673287633543e-09)
    t = s + s
    return 1.0 - t * s, t * c


def split(x):
    hi = x.astype(BF16)
    return hi, (x - hi.astype(F32)).astype(BF16)


def mm(a, b, nt=False):
    dims = (((1,), (1 if nt else 0,)), ((), ()))
    return lax.dot_general(a, b, dims, preferred_element_type=F32)


def rotate(a_re, a_im, b_re, b_im):
    return a_re * b_re - a_im * b_im, a_re * b_im + a_im * b_re


def put(hi_ref, lo_ref, at, size, col, x):
    hi, lo = split(x)
    hi_ref[pl.ds(at, size), col : col + BAND] = hi
    lo_ref[pl.ds(at, size), col : col + BAND] = lo
    return hi, lo


def multiply_band(n_col, t, table, field, a_re, a_im, b_re, b_im, out):
    rows = field.shape[0] // 2
    cols = field.shape[1]
    part = BAND // (n_col * CHUNKS)
    per = part // STEP
    for j in range(0, cols, LANES):
        br = b_re[:, j : j + LANES]
        bi = b_im[:, j : j + LANES]
        for h in range(CHUNKS):
            for i in range(per):
                row = (t * CHUNKS + h) * per + i
                re, im = rotate(a_re[row : row + 1, j : j + LANES], a_im[row : row + 1, j : j + LANES], br, bi)
                at = 2 * h * part + i * STEP
                table[at : at + STEP, j : j + LANES] = re.astype(BF16)
                table[at + part : at + part + STEP, j : j + LANES] = im.astype(BF16)
    prod = mm(table[...], field[...], nt=True)
    for at in range(0, 2 * CHUNKS * part, 2 * part):
        mid = at + part
        out[at:mid, :] = prod[at:mid, :rows] - prod[mid : mid + part, rows:]
        out[mid : mid + part, :] = prod[at:mid, rows:] + prod[mid : mid + part, :rows]


def first_kernel(n_col, offs_hbm, ph_hbm, out, field, a_re, a_im, b_re, b_im, ph, offs, table, sem, ph_sem):
    rows, cols = ph.shape
    pieces = ph_sem.shape[0]
    size = rows // pieces
    get = pltpu.make_async_copy(offs_hbm, offs, sem)
    get.start()
    loads = [
        pltpu.make_async_copy(ph_hbm.at[pl.ds(i * size, size)], ph.at[pl.ds(i * size, size)], ph_sem.at[i])
        for i in range(pieces)
    ]
    for load in loads:
        load.start()
    me = lax.axis_index("col")
    n0 = me * cols
    share = BAND // n_col
    per = share // STEP
    for j in range(0, cols, LANES):
        n = n0 + j + lax.broadcasted_iota(I32, (BAND // STEP, LANES), 1)
        row = lax.broadcasted_iota(I32, (BAND // STEP, LANES), 0)
        v = (me ^ (row // per)) * share + (row % per) * STEP
        c, s = circle((v * n) & (HOLO - 1), HOLO)
        a_re[:, j : j + LANES] = c
        a_im[:, j : j + LANES] = -s
    get.wait()
    offset = offs[0, 1]
    for j in range(0, cols, LANES):
        n = n0 + j + lax.broadcasted_iota(I32, (STEP, LANES), 1)
        low = lax.broadcasted_iota(I32, (STEP, LANES), 0)
        c, s = circle((((offset + low) & (HOLO - 1)) * n) & (HOLO - 1), HOLO)
        b_re[:, j : j + LANES] = c
        b_im[:, j : j + LANES] = -s
    for i in range(pieces):
        loads[i].wait()
        for at in range(i * size, (i + 1) * size, STEP):
            for j in range(0, cols, LANES):
                c, s = radians(ph[at : at + STEP, j : j + LANES])
                field[at : at + STEP, j : j + LANES] = c.astype(BF16)
                field[rows + at : rows + at + STEP, j : j + LANES] = s.astype(BF16)
    multiply_band(n_col, n_col - 1, table, field, a_re, a_im, b_re, b_im, out)


def later_kernel(n_col, t, field, a_re, a_im, b_re, b_im, out, table):
    multiply_band(n_col, t, table, field, a_re, a_im, b_re, b_im, out)


def lens_table_kernel(
    n_row, n_col, n_pupil, spacing, offs_hbm, codes_hbm, fl_hi, fl_lo, lens_hi, lens_lo, ev, a_re, a_im, offs, codes, sems
):
    gets = [
        pltpu.make_async_copy(offs_hbm, offs, sems.at[0]),
        pltpu.make_async_copy(codes_hbm, codes, sems.at[1]),
    ]
    for get in gets:
        get.start()
    depths = codes.shape[0]
    r, c, p = (lax.axis_index(a) for a in ("row", "col", "pupil"))
    own = depths // n_pupil
    xs = BAND // (n_row * n_col)
    share = BAND // n_col
    part = share // CHUNKS
    big = 4 * (BAND // 2) ** 2
    scale = 1.0 / math.sqrt(BAND)
    for get in gets:
        get.wait()
    offset = offs[0, 0]
    rows_here = fl_hi.shape[0] // n_row
    per = rows_here // STEP
    blocks = a_re.shape[0]
    row = lax.broadcasted_iota(I32, (blocks, BAND), 0)
    freq = (offset + lax.broadcasted_iota(I32, (blocks, BAND), 1)) & (HOLO - 1)
    m = (r ^ (row // per)) * rows_here + (row % per) * STEP
    cs, sn = circle((freq * (m * spacing)) & (HOLO - 1), HOLO)
    a_re[...] = cs
    a_im[...] = -sn
    low = lax.broadcasted_iota(I32, (STEP, BAND), 0)
    freq = (offset + lax.broadcasted_iota(I32, (STEP, BAND), 1)) & (HOLO - 1)
    b_re, b_im = circle((freq * (low * spacing)) & (HOLO - 1), HOLO)
    b_im = -b_im

    def fill(i, _):
        at = pl.multiple_of(i * STEP, STEP)
        re, im = rotate(a_re[pl.ds(i, 1), :], a_im[pl.ds(i, 1), :], b_re, b_im)
        put(fl_hi, fl_lo, at, STEP, 0, re)
        put(fl_hi, fl_lo, at, STEP, BAND, im)
        return 0

    lax.fori_loop(0, blocks, fill, 0, unroll=4)
    code = [codes[((d // own) ^ p) * own + d % own] for d in range(depths)]
    u = lax.broadcasted_iota(I32, (1, BAND), 1) - BAND // 2
    turn = [circle((code[d] * (u * u)) & (big - 1), big) for d in range(depths)]
    for t in range(n_col):
        x = (r * n_col + (c ^ t)) * xs + lax.broadcasted_iota(I32, (xs, BAND), 0)
        uu = lax.broadcasted_iota(I32, (xs, BAND), 1)
        g_re, g_im = circle((x * uu) & (BAND - 1), BAND)
        g_re = g_re * scale
        g_im = g_im * scale
        for d in range(depths):
            re, im = rotate(g_re, g_im, *turn[d])
            at = (t * depths + d) * xs
            put(lens_hi, lens_lo, at, xs, 0, re)
            put(lens_hi, lens_lo, at, xs, BAND, im)
    lane = lax.broadcasted_iota(I32, (1, 2 * part), 1)
    for h in range(CHUNKS):
        v = c * share + h * part + lane % part - BAND // 2
        for d in range(depths):
            e_re, e_im = circle((code[d] * (v * v)) & (big - 1), big)
            at = 2 * (h * depths + d)
            ev[at : at + 1, :] = e_re
            ev[at + 1 : at + 2, :] = jnp.where(lane < part, -e_im, e_im)


def image_table_kernel(n_col, *refs):
    c = lax.axis_index("col")
    share = BAND // n_col
    part = share // CHUNKS
    per = part // STEP
    scale = 1.0 / math.sqrt(BAND)
    a_re, a_im = refs[2 * CHUNKS :]
    row = lax.broadcasted_iota(I32, a_re.shape, 0)
    y = lax.broadcasted_iota(I32, a_re.shape, 1)
    v = (c ^ ((row // per) % n_col)) * share + (row // (per * n_col)) * part + (row % per) * STEP
    cs, sn = circle((v * y) & (BAND - 1), BAND)
    a_re[...] = cs
    a_im[...] = sn
    low = lax.broadcasted_iota(I32, (STEP, BAND), 0)
    y = lax.broadcasted_iota(I32, (STEP, BAND), 1)
    b_re, b_im = circle((low * y) & (BAND - 1), BAND)
    b_re = b_re * scale
    b_im = b_im * scale
    for h in range(CHUNKS):
        g_hi, g_lo = refs[2 * h : 2 * h + 2]
        for t in range(n_col):
            for i in range(per):
                row = (h * n_col + t) * per + i
                re, im = rotate(a_re[row : row + 1, :], a_im[row : row + 1, :], b_re, b_im)
                at = 2 * t * part + i * STEP
                hi, lo = put(g_hi, g_lo, at, STEP, 0, re)
                g_hi[at + part : at + part + STEP, BAND:] = hi
                g_lo[at + part : at + part + STEP, BAND:] = lo
                hi, lo = put(g_hi, g_lo, at, STEP, BAND, im)
                g_hi[at + part : at + part + STEP, :BAND] = -hi
                g_lo[at + part : at + part + STEP, :BAND] = -lo


def turn_and_send(n_row, n_col, depths, chunk, t, lens_hi, lens_lo, ev, w2, out):
    part = BAND // (n_col * CHUNKS)
    both = 2 * part
    xs = BAND // (n_row * n_col)
    block = depths * xs
    at = t * block
    z = mm(lens_hi[at : at + block, :], w2[...], nt=True)
    z = z[:, :both] + (z[:, both:] + mm(lens_lo[at : at + block, :], w2[:both, :], nt=True))
    for d in range(depths):
        piece = z[d * xs : (d + 1) * xs, :]
        row = 2 * (chunk * depths + d)
        turned = piece * ev[row : row + 1, :] + pltpu.roll(piece, part, 1) * ev[row + 1 : row + 2, :]
        out[d * xs : (d + 1) * xs, :] = turned


def lens_kernel(n_row, n_col, depths, chunk, *refs):
    halves = refs[:n_row]
    fl_hi, fl_lo, lens_hi, lens_lo, ev = refs[n_row : n_row + 5]
    outs = refs[n_row + 5 : n_row + 4 + n_col]
    w2, x2 = refs[n_row + 4 + n_col :]
    part = BAND // (n_col * CHUNKS)
    both = 2 * part
    rows_here = halves[0].shape[1]
    for i, h in enumerate(halves):
        hi, lo = split(h[...])
        x2[:both, i * rows_here : (i + 1) * rows_here] = hi
        x2[both:, i * rows_here : (i + 1) * rows_here] = lo
    s = mm(x2[...], fl_hi[...])
    s = s[:both] + (s[both:] + mm(x2[:both, :], fl_lo[...]))
    s_re = (s[:part, :BAND] - s[part:, BAND:]) * (1.0 / HOLO)
    s_im = (s[:part, BAND:] + s[part:, :BAND]) * (1.0 / HOLO)
    hi, lo = split(s_re)
    w2[:part, :BAND] = hi
    w2[part:both, BAND:] = hi
    w2[both : both + part, :BAND] = lo
    w2[both + part :, BAND:] = lo
    hi, lo = split(s_im)
    w2[part:both, :BAND] = hi
    w2[:part, BAND:] = -hi
    w2[both + part :, :BAND] = lo
    w2[both : both + part, BAND:] = -lo
    for t in range(n_col - 1, 0, -1):
        turn_and_send(n_row, n_col, depths, chunk, t, lens_hi, lens_lo, ev, w2, outs[t - 1])


def own_lens_kernel(n_row, n_col, depths, chunk, *refs):
    turn_and_send(n_row, n_col, depths, chunk, 0, *refs)


def image_sum(blocks, g_hi, g_lo):
    hi, lo = split(jnp.concatenate(blocks, axis=1))
    return mm(hi, g_hi[...]) + (mm(lo, g_hi[...]) + mm(hi, g_lo[...]))


def image_kernel(n_col, *refs):
    refs[-1][...] = image_sum([x[...] for x in refs[:n_col]], refs[n_col], refs[n_col + 1])


def power_kernel(n_col, lo_rows, hi_rows, *refs):
    z = image_sum([x[lo_rows:hi_rows, :] for x in refs[:n_col]], refs[n_col], refs[n_col + 1])
    for more in refs[n_col + 2 : -1]:
        z = z + more[lo_rows:hi_rows, :]
    re = z[:, :BAND]
    im = z[:, BAND:]
    refs[-1][...] = re * re + im * im


def spec(shape, dtype=F32):
    return jax.ShapeDtypeStruct(shape, dtype)


def call(kernel, outs, ins, scratch=(), hbm=0, mib=16):
    vm = pl.BlockSpec(memory_space=pltpu.VMEM)
    return pl.pallas_call(
        kernel,
        out_shape=outs,
        in_specs=[pl.BlockSpec(memory_space=pltpu.HBM)] * hbm + [vm] * (ins - hbm),
        out_specs=[vm] * len(outs),
        scratch_shapes=list(scratch),
        compiler_params=pltpu.CompilerParams(vmem_limit_bytes=mib * 1024 * 1024),
    )


def in_hbm(x):
    return pltpu.with_memory_space_constraint(x, pltpu.HBM)


def swap(x, axis, t):
    n = lax.axis_size(axis)
    return lax.ppermute(x, axis, [(i, i ^ t) for i in range(n)])


def local(phase, band_offsets, depth_codes):
    rows, cols = phase.shape
    n_row, n_col, n_pupil = (lax.axis_size(a) for a in ("row", "col", "pupil"))
    depths = depth_codes.shape[0]
    own = depths // n_pupil
    share = BAND // n_col
    part = share // CHUNKS
    xs = BAND // (n_row * n_col)
    block = depths * xs
    spacing = HOLO // (rows * n_row)
    dma = pltpu.SemaphoreType.DMA

    piece = spec((2 * share, rows))
    table = pltpu.VMEM((2 * share, cols), BF16)
    offs = in_hbm(band_offsets)
    first = call(
        functools.partial(first_kernel, n_col),
        [piece, spec((2 * rows, cols), BF16)] + [spec((BAND // STEP, cols))] * 2 + [spec((STEP, cols))] * 2,
        2,
        [pltpu.VMEM((rows, cols), F32), pltpu.SMEM(band_offsets.shape, I32), table, dma, dma((4,))],
        2,
    )(offs, in_hbm(phase))
    got = [swap(first[0], "col", n_col - 1)]
    for t in range(n_col - 2, -1, -1):
        x = call(functools.partial(later_kernel, n_col, t), [piece], 5, [table])(*first[1:])[0]
        got.append(swap(x, "col", t) if t else x)

    blocks = n_row * rows // STEP
    lens_tables = call(
        functools.partial(lens_table_kernel, n_row, n_col, n_pupil, spacing),
        [spec((n_row * rows, 2 * BAND), BF16)] * 2
        + [spec((n_col * block, 2 * BAND), BF16)] * 2
        + [spec((2 * CHUNKS * depths, 2 * part))],
        2,
        [pltpu.VMEM((blocks, BAND), F32)] * 2
        + [pltpu.SMEM(band_offsets.shape, I32), pltpu.SMEM(depth_codes.shape, I32), dma((2,))],
        2,
    )
    tables = lens_tables(offs, in_hbm(depth_codes))
    image_tables = call(
        functools.partial(image_table_kernel, n_col),
        [spec((2 * n_col * part, 2 * BAND), BF16)] * (2 * CHUNKS),
        0,
        [pltpu.VMEM((BAND // STEP, BAND), F32)] * 2,
    )()

    sums = []
    blocks = []
    for h in range(CHUNKS):
        half = got[-1][2 * h * part : 2 * (h + 1) * part]
        for x in got[:-1]:
            half = half + x[2 * h * part : 2 * (h + 1) * part]
        halves = [half] + [swap(half, "row", t) for t in range(1, n_row)]
        piece = spec((block, 2 * part))
        *lens, w2 = call(
            functools.partial(lens_kernel, n_row, n_col, depths, h),
            [piece] * (n_col - 1) + [spec((4 * part, 2 * BAND), BF16)],
            n_row + 5,
            [pltpu.VMEM((4 * part, n_row * rows), BF16)],
        )(*halves, *tables)
        own_lens = call(functools.partial(own_lens_kernel, n_row, n_col, depths, h), [piece], 4)(*tables[2:], w2)
        arrived = [swap(lens[t - 1], "col", t) for t in range(n_col - 1, 0, -1)]
        blocks.append(list(own_lens) + arrived[::-1])
    for h in range(CHUNKS - 1):
        sums += call(functools.partial(image_kernel, n_col), [spec((block, 2 * BAND))], n_col + 2)(
            *blocks[h], *image_tables[2 * h : 2 * h + 2]
        )
    size = block // n_pupil
    power = {}
    for t in list(range(1, n_pupil)) + [0]:
        power[t] = call(
            functools.partial(power_kernel, n_col, t * size, (t + 1) * size),
            [spec((size, BAND))],
            n_col + 2 + len(sums),
        )(*blocks[-1], *image_tables[-2:], *sums)[0]
    received = [swap(power[t], "pupil", t) for t in range(1, n_pupil)]
    total = power[0]
    for x in received:
        total = total + x
    total = total * (1.0 / (band_offsets.shape[0] * n_pupil))
    return total.reshape(own, xs, BAND)


def solution(mesh):
    in_specs = (P("row", "col"), P("pupil", None), P())
    out_specs = P("pupil", ("row", "col"), None)
    return jax.shard_map(local, mesh=mesh, in_specs=in_specs, out_specs=out_specs, check_vma=False)
```
